32 devices in a mesh: groups: 2 (over x), expert: 16 (over z, y, core).
Axes of the slice: x: 2, y: 2, z: 4, core: 2. Of those that a mesh axis runs over, the one named last changes fastest.
Arguments:
- tokens: bfloat16 [256, 6144], P(('groups', 'expert')), parts along dimension 0, may hold values from -6 to 6
- norm_gain: float32 [6144], replicated, may hold values from 0.5 to 1.5
- router: bfloat16 [6144, 4], replicated, may hold values from -0.078125 to 0.078125
- w_gate: bfloat16 [6144, 4096], P(None, 'expert'), may hold values from -0.078125 to 0.078125
- w_up: bfloat16 [6144, 4096], P(None, 'expert'), may hold values from -0.078125 to 0.078125
- w_down: bfloat16 [4096, 6144], P('expert'), may hold values from -0.1875 to 0.1875
- expert_ids: int32 [256, 2], P(('groups', 'expert')), parts along dimension 0, may hold values from 0 to 3, as said below
- live_rows: int32 [32], P(('groups', 'expert')), parts along dimension 0, may hold values from 6 to 8, as said below
Outputs:
- mixed_out: bfloat16 [256, 6144], P(('groups', 'expert')), parts along dimension 0
The draws below stay inside these ranges and needn't reach their ends.
There are 2 independent parts, one for each index of `groups`. The reference program is written for one: setup_inputs(seed, part) draws one part's arguments, and reference() takes and returns one part's arrays. A program takes and returns all parts, laid end to end along the dimension named above; an argument that names none is the same for every part. Nothing has to cross between parts.
Inputs may be any that keep to these rules, and one draw needn't show every extreme that they name: `expert_ids`: each row names two different experts. Among the live rows of one device no expert is named by more than 6 rows; in every draw some expert is named by exactly 6 live rows of every device. `live_rows`: rows at or beyond this count in a device's block are padding; some device is full in every draw.
All inputs are finite; a program needn't handle non-finite values.
Results may differ from the reference program's by a relative error of at most 0.0042.
Values may be sent and summed in bfloat16 or wider, within the bound.
A program may use at most 128 MiB of HBM per device.

```python
import jax
import jax.numpy as jnp
from jax import lax

D = 6144
EXPERTS = 4
FF_DEV = 256
B_DEV = 8
CAP = 6
FF = 1024
TOKENS = 128
N_EXPERT = 16


def routing_tables(key):
    base = jax.random.fold_in(key, 23)
    keys = jax.random.split(base, 6)
    hot = jax.random.randint(keys[0], (), 0, EXPERTS)
    live_count = jax.random.randint(keys[1], (N_EXPERT,), CAP, B_DEV + 1)
    full_device = jax.random.randint(keys[2], (), 0, N_EXPERT)
    live_count = jnp.where(jnp.arange(N_EXPERT) == full_device, B_DEV, live_count)
    shifted = jax.random.randint(keys[3], (N_EXPERT,), 0, B_DEV) % live_count
    offset = jax.random.randint(keys[4], (N_EXPERT, 1), 0, EXPERTS - 1)
    flipped = jax.random.randint(keys[5], (N_EXPERT, B_DEV), 0, 2)
    rank = (jnp.arange(B_DEV)[None, :] + shifted[:, None]) % live_count[:, None]
    spare = EXPERTS - 1
    first_other = (hot + 1 + (offset + rank) % spare) % EXPERTS
    second_other = (hot + 1 + (offset + rank + 1) % spare) % EXPERTS
    leading = jnp.where(rank < CAP, hot, first_other)
    trailing = jnp.where(rank < CAP, first_other, second_other)
    first_pick = jnp.where(flipped == 1, trailing, leading)
    second_pick = jnp.where(flipped == 1, leading, trailing)
    chosen_ids = jnp.stack([first_pick, second_pick], axis=-1).reshape(N_EXPERT * B_DEV, 2)
    return (chosen_ids.astype(jnp.int32), live_count.astype(jnp.int32))


def draw_expert_ids(key, part):
    return routing_tables(key)[0]


def draw_live_rows(key, part):
    return routing_tables(key)[1]


def level_of(stream_key, dims, shards, smallest, largest):
    factor_of = 1.0
    for axis_at, parts in shards:
        steps = jax.random.uniform(jax.random.fold_in(jax.random.fold_in(stream_key, 6), axis_at), (parts,), jnp.float32, smallest / len(shards), largest / len(shards))
        factor_of = factor_of * jnp.repeat(jnp.exp(steps), dims[axis_at] // parts).reshape((-1,) + (1,) * (len(dims) - 1 - axis_at))
    return factor_of


def scatter_about(stream_key, dims, width, limit, cuts=(), kind=jnp.bfloat16):
    loudness = level_of(stream_key, dims, cuts, -0.22, 0.18) if cuts else 1.0
    result = jax.random.normal(stream_key, dims, jnp.float32) * width * loudness
    return jnp.minimum(jnp.maximum(result, -limit), limit).astype(kind)


def setup_inputs(seed: int = 0, part: int = 0) -> dict:
    seeds = jax.random.split(jax.random.key(seed), 9)
    part_splits = jax.random.split(jax.random.fold_in(seeds[8], part), 9)
    return {
        "tokens": scatter_about(part_splits[0], (TOKENS, D), 1.0, 6.0, ((0, 16),)),
        "norm_gain": jnp.clip(1.0 + 0.1 * jax.random.normal(seeds[1], (D,), jnp.float32), 0.5, 1.5),
        "router": scatter_about(seeds[2], (D, EXPERTS), D ** -0.5, 0.078125),
        "w_gate": scatter_about(seeds[3], (D, EXPERTS * FF), D ** -0.5, 0.078125, ((1, 16),)),
        "w_up": scatter_about(seeds[4], (D, EXPERTS * FF), D ** -0.5, 0.078125, ((1, 16),)),
        "w_down": scatter_about(seeds[5], (EXPERTS * FF, D), FF ** -0.5, 0.1875, ((0, 16),)),
        "expert_ids": draw_expert_ids(jax.random.fold_in(jax.random.fold_in(seeds[8], part), 71), part),
        "live_rows": draw_live_rows(jax.random.fold_in(jax.random.fold_in(seeds[8], part), 71), part),
    }


epsilon = 1e-05

def rms_normed(tokens, norm_gain):
    tok_f32 = tokens.astype(jnp.float32)
    scale_inv = lax.rsqrt(lax.optimization_barrier(jnp.mean(tok_f32 * tok_f32, axis=-1, keepdims=True)) + epsilon)
    return (tok_f32 * scale_inv * norm_gain).astype(jnp.bfloat16)

def add_block(running, block_pair):
    partial_value = jnp.dot(block_pair[0], block_pair[1], preferred_element_type=jnp.float32).astype(jnp.bfloat16)
    partial_value = lax.optimization_barrier(partial_value)
    return (running + partial_value.astype(jnp.float32), None)

def reference(tokens, norm_gain, router, w_gate, w_up, w_down, expert_ids, live_rows):
    normed = rms_normed(tokens, norm_gain)
    logits = jnp.dot(normed, router, preferred_element_type=jnp.float32)
    one_hot = (expert_ids[:, :, None] == jnp.arange(EXPERTS, dtype=jnp.int32)[None, None, :]).astype(jnp.float32)
    chosen = lax.optimization_barrier(jnp.sum(one_hot * logits[:, None, :], axis=-1))
    gate_probs = jax.nn.sigmoid(chosen - chosen[:, ::-1])
    positions = jnp.arange(TOKENS, dtype=jnp.int32)
    alive_mask = (positions % B_DEV < live_rows[positions // B_DEV]).astype(jnp.float32)
    expert_weight = lax.optimization_barrier(jnp.sum(one_hot * (gate_probs * alive_mask[:, None])[:, :, None], axis=1))
    members = FF // FF_DEV
    routed_out = jnp.zeros((TOKENS, D), jnp.float32)
    for expert in range(EXPERTS):
        gate_proj = jnp.dot(normed, w_gate[:, expert * FF:(expert + 1) * FF], preferred_element_type=jnp.float32)
        up_proj = jnp.dot(normed, w_up[:, expert * FF:(expert + 1) * FF], preferred_element_type=jnp.float32)
        hidden = (jax.nn.silu(gate_proj) * up_proj).astype(jnp.bfloat16)
        blocks_hidden = hidden.reshape(TOKENS, members, FF_DEV).transpose(1, 0, 2)
        blocks_down = w_down[expert * FF:(expert + 1) * FF].reshape(members, FF_DEV, D)
        expert_out, unused = lax.scan(add_block, jnp.zeros((TOKENS, D), jnp.float32), (blocks_hidden, blocks_down))
        routed_out = routed_out + expert_weight[:, expert:expert + 1] * expert_out
    return (tokens.astype(jnp.float32) + routed_out).astype(jnp.bfloat16)
```

```python
import functools

import jax
import jax.numpy as jnp
from jax import lax
from jax.experimental import pallas as pl
from jax.experimental.pallas import tpu as pltpu
from jax.sharding import PartitionSpec as P

EPS = 1e-05
LANES = 128
GATHER_CHUNKS = 4
REDUCE_CHUNKS = 4
ROW_BLOCK = 128
CORES = 2


def _mod(a, n):
    return lax.rem(a + n, n)


def kernel(
    E, Q, B, D, H,
    live_ref, tok_hbm, gain_ref, router_ref, ids_ref, wg_hbm, wu_hbm, wd_hbm,
    out_ref,
    tok_ref, G, wg, wu, wd, acc_g, acc_u, hid, part, core_in, chip_sum, quad_in, plane, plane_in,
    load_sem, az_send, az_recv, aq_send, aq_recv, ac_send, ac_recv,
    rc_send, rc_recv, rq_send, rq_recv, rz_send, rz_recv,
):
    me = lax.axis_index("expert")
    members = Q * CORES
    e = me // members
    m = lax.rem(me, members)
    q = m // CORES
    c = lax.rem(m, CORES)
    rows = CORES * Q * E * B
    half = Q * E * B
    quad = E * B

    def dev(e_, q_, c_):
        return {"expert": (e_ * Q + q_) * CORES + c_}

    def slot(e_, q_, c_):
        return (c_ * Q + q_) * E + e_

    def remote(src, dst, ssem, rsem, device):
        return pltpu.make_async_remote_copy(
            src_ref=src, dst_ref=dst, send_sem=ssem, recv_sem=rsem,
            device_id=device, device_id_type=pl.DeviceIdType.MESH,
        )

    def wait_bytes(ref, sem):
        pltpu.make_async_copy(ref, ref, sem).wait()

    barrier = pltpu.get_barrier_semaphore()
    others_e = [_mod(e + d, E) for d in range(1, E)]
    others_q = [_mod(q + d, Q) for d in range(1, Q)]
    for e2 in others_e:
        pl.semaphore_signal(barrier, inc=1, device_id=dev(e2, q, c), device_id_type=pl.DeviceIdType.MESH)
    for q2 in others_q:
        pl.semaphore_signal(barrier, inc=1, device_id=dev(e, q2, c), device_id_type=pl.DeviceIdType.MESH)
    pl.semaphore_signal(barrier, inc=1, device_id=dev(e, q, 1 - c), device_id_type=pl.DeviceIdType.MESH)

    tok_load = pltpu.make_async_copy(tok_hbm, tok_ref, load_sem.at[0])
    wg_load = pltpu.make_async_copy(wg_hbm, wg, load_sem.at[1])
    wu_load = pltpu.make_async_copy(wu_hbm, wu, load_sem.at[2])
    wd_load = pltpu.make_async_copy(wd_hbm, wd, load_sem.at[3])
    tok_load.start()
    wg_load.start()
    wu_load.start()
    wd_load.start()
    tok_load.wait()

    tok = tok_ref[...].astype(jnp.float32)
    scale = lax.rsqrt(jnp.sum(tok * tok, axis=-1, keepdims=True) * (1.0 / D) + EPS)
    normed = (tok * scale * gain_ref[...]).astype(jnp.bfloat16)
    mine = slot(e, q, c)
    G[mine, :, :D] = normed

    pl.semaphore_wait(barrier, (E - 1) + (Q - 1) + 1)

    step = D // GATHER_CHUNKS
    spans = [
        pl.ds(j * step, step + (LANES if j == GATHER_CHUNKS - 1 else 0))
        for j in range(GATHER_CHUNKS)
    ]

    def send_experts(j):
        for d in range(1, E):
            view = G.at[mine, :, spans[j]]
            remote(view, view, az_send, az_recv.at[j, d - 1], dev(others_e[d - 1], q, c)).start()

    for j in range(GATHER_CHUNKS - 1):
        send_experts(j)

    normed_f = normed.astype(jnp.float32)
    router = router_ref[...].astype(jnp.float32)
    ids = ids_ref[...]
    first_id, second_id = ids[:, 0:1], ids[:, 1:2]
    first = jnp.zeros((B, 1), jnp.float32)
    second = jnp.zeros((B, 1), jnp.float32)
    for k in range(E):
        logit = jnp.sum(normed_f * router[k : k + 1, :], axis=-1, keepdims=True)
        first = jnp.where(first_id == k, logit, first)
        second = jnp.where(second_id == k, logit, second)
    row_at = lax.broadcasted_iota(jnp.int32, (B, 1), 0)
    alive = jnp.where(row_at < live_ref[0], 1.0, 0.0).astype(jnp.float32)
    gate0 = alive * jax.nn.sigmoid(first - second)
    gate1 = alive * jax.nn.sigmoid(second - first)
    lane = lax.broadcasted_iota(jnp.int32, (B, LANES), 1)
    low_lane = lane - E
    weight = jnp.where(first_id == lane, gate0, 0.0) + jnp.where(second_id == lane, gate1, 0.0)
    again = jnp.where(first_id == low_lane, gate0, 0.0) + jnp.where(second_id == low_lane, gate1, 0.0)
    low = again - again.astype(jnp.bfloat16).astype(jnp.float32)
    G[mine, :, pl.ds(D, LANES)] = (weight + low).astype(jnp.bfloat16)
    send_experts(GATHER_CHUNKS - 1)

    def gather_a(j):
        for d in range(E):
            s = slot(_mod(e - d, E), q, c)
            view = G.at[s, :, spans[j]]
            if d:
                remote(view, view, az_send, az_recv.at[j, d - 1], dev(e, q, c)).wait_recv()
            for dq in range(1, Q):
                remote(view, view, aq_send, aq_recv.at[j, dq - 1], dev(e, others_q[dq - 1], c)).start()
        view = G.at[pl.ds(slot(0, q, c), E), :, spans[j]]
        remote(view, view, ac_send, ac_recv.at[j, 0], dev(e, q, 1 - c)).start()

    def gather_b(j):
        for dq in range(1, Q):
            view = G.at[pl.ds(slot(0, _mod(q - dq, Q), c), E), :, spans[j]]
            wait_bytes(view, aq_recv.at[j, dq - 1])
            remote(view, view, ac_send, ac_recv.at[j, dq], dev(e, q, 1 - c)).start()

    blocks = max(1, rows // ROW_BLOCK)
    block = rows // blocks

    def over_rows(body):
        if blocks == 1:
            body(0)
        else:
            lax.fori_loop(0, blocks, lambda i, _: (body(i), 0)[1], 0)

    def lhs(i, at, width):
        view = G[pl.ds(i * (block // B), block // B), :, pl.ds(at, width)]
        return view.astype(jnp.float32).reshape(block, width)

    def gather_c(j):
        for dq in range(Q):
            view = G.at[pl.ds(slot(0, _mod(q - dq, Q), 1 - c), E), :, spans[j]]
            wait_bytes(view, ac_recv.at[j, dq])
        if j == 0:
            wg_load.wait()
            wu_load.wait()

        def body(i):
            at = pl.ds(i * block, block)
            x = lhs(i, j * step, step).astype(jnp.bfloat16)
            g = jnp.dot(x, wg[pl.ds(j * step, step), :], preferred_element_type=jnp.float32)
            u = jnp.dot(x, wu[pl.ds(j * step, step), :], preferred_element_type=jnp.float32)
            if j:
                g = g + acc_g[at, :]
                u = u + acc_u[at, :]
            if j < GATHER_CHUNKS - 1:
                acc_g[at, :] = g
                acc_u[at, :] = u
            else:
                coded = lhs(i, D, LANES)
                lanes = lax.broadcasted_iota(jnp.int32, coded.shape, 1)
                keep = (lanes == e) | (lanes == e + E)
                w = jnp.sum(jnp.where(keep, coded, 0.0), axis=-1, keepdims=True)
                hid[at, :] = (g / (1.0 + jnp.exp(-g)) * u * w).astype(jnp.bfloat16)

        over_rows(body)

    for t in range(GATHER_CHUNKS + 2):
        if t < GATHER_CHUNKS:
            gather_a(t)
        if 0 <= t - 1 < GATHER_CHUNKS:
            gather_b(t - 1)
        if 0 <= t - 2 < GATHER_CHUNKS:
            gather_c(t - 2)

    wd_load.wait()
    width = D // REDUCE_CHUNKS

    def at_rows(start, size):
        return pl.ds(pl.multiple_of(start, 16), size)

    def reduce_a(j):
        cols = pl.ds(j * width, width)

        def body(i):
            at = pl.ds(i * block, block)
            part[at, cols] = jnp.dot(
                hid[at, :], wd[:, cols], preferred_element_type=jnp.float32
            ).astype(jnp.bfloat16)

        over_rows(body)
        remote(
            part.at[at_rows((1 - c) * half, half), cols], core_in.at[:, cols],
            rc_send, rc_recv.at[j], dev(e, q, 1 - c),
        ).start()

    def reduce_b(j):
        cols = pl.ds(j * width, width)
        wait_bytes(core_in.at[:, cols], rc_recv.at[j])
        for d in list(range(1, Q)) + [0]:
            q2 = _mod(q + d, Q)
            at = at_rows(q2 * quad, quad)
            own = part[at_rows(c * half + q2 * quad, quad), cols].astype(jnp.float32)
            chip_sum[at, cols] = (own + core_in[at, cols].astype(jnp.float32)).astype(jnp.bfloat16)
            if d:
                remote(
                    chip_sum.at[at, cols], quad_in.at[d - 1, :, cols],
                    rq_send, rq_recv.at[j, d - 1], dev(e, q2, c),
                ).start()

    def reduce_c(j):
        cols = pl.ds(j * width, width)
        total = chip_sum[at_rows(q * quad, quad), cols].astype(jnp.float32)
        for d in range(1, Q):
            wait_bytes(quad_in.at[d - 1, :, cols], rq_recv.at[j, d - 1])
            total = total + quad_in[d - 1, :, cols].astype(jnp.float32)
        plane[:, :, cols] = total.reshape(E, B, width).astype(jnp.bfloat16)
        for d in range(1, E):
            remote(
                plane.at[others_e[d - 1], :, cols], plane_in.at[d - 1, :, cols],
                rz_send, rz_recv.at[j, d - 1], dev(others_e[d - 1], q, c),
            ).start()

    def reduce_d(j):
        cols = pl.ds(j * width, width)
        total = tok_ref[:, cols].astype(jnp.float32) + plane[e, :, cols].astype(jnp.float32)
        for d in range(1, E):
            wait_bytes(plane_in.at[d - 1, :, cols], rz_recv.at[j, d - 1])
            total = total + plane_in[d - 1, :, cols].astype(jnp.float32)
        out_ref[:, cols] = total.astype(jnp.bfloat16)

    for t in range(REDUCE_CHUNKS + 3):
        for lag, stage in enumerate((reduce_a, reduce_b, reduce_c, reduce_d)):
            if 0 <= t - lag < REDUCE_CHUNKS:
                stage(t - lag)

    wait_bytes(G.at[pl.ds(0, E - 1)], az_send)
    if Q > 1:
        wait_bytes(G.at[pl.ds(0, (Q - 1) * E)], aq_send)
    wait_bytes(G.at[pl.ds(0, Q * E)], ac_send)
    wait_bytes(core_in, rc_send)
    if Q > 1:
        wait_bytes(quad_in, rq_send)
    wait_bytes(plane_in, rz_send)


def local(tokens, norm_gain, router, w_gate, w_up, w_down, expert_ids, live_rows):
    devices = lax.axis_size("expert")
    B, D = tokens.shape
    E = router.shape[1]
    H = w_gate.shape[1]
    Q = devices // E // CORES
    rows = devices * B
    bf = jnp.bfloat16
    vmem = pl.BlockSpec(memory_space=pltpu.VMEM)
    anyspace = pl.BlockSpec(memory_space=pl.ANY)
    dma = pltpu.SemaphoreType.DMA
    return pl.pallas_call(
        functools.partial(kernel, E, Q, B, D, H),
        out_shape=jax.ShapeDtypeStruct((B, D), bf),
        in_specs=[
            pl.BlockSpec(memory_space=pltpu.SMEM),
            anyspace, vmem, vmem, vmem, anyspace, anyspace, anyspace,
        ],
        out_specs=vmem,
        scratch_shapes=[
            pltpu.VMEM((B, D), bf),
            pltpu.VMEM((devices, B, D + LANES), bf),
            pltpu.VMEM((D, H), bf),
            pltpu.VMEM((D, H), bf),
            pltpu.VMEM((H, D), bf),
            pltpu.VMEM((rows, H), jnp.float32),
            pltpu.VMEM((rows, H), jnp.float32),
            pltpu.VMEM((rows, H), bf),
            pltpu.VMEM((rows, D), bf),
            pltpu.VMEM((Q * E * B, D), bf),
            pltpu.VMEM((Q * E * B, D), bf),
            pltpu.VMEM((max(Q - 1, 1), E * B, D), bf),
            pltpu.VMEM((E, B, D), bf),
            pltpu.VMEM((E - 1, B, D), bf),
            dma((4,)),
            dma, dma((GATHER_CHUNKS, E - 1)),
            dma, dma((GATHER_CHUNKS, max(Q - 1, 1))),
            dma, dma((GATHER_CHUNKS, Q)),
            dma, dma((REDUCE_CHUNKS,)),
            dma, dma((REDUCE_CHUNKS, max(Q - 1, 1))),
            dma, dma((REDUCE_CHUNKS, E - 1)),
        ],
        compiler_params=pltpu.CompilerParams(
            collective_id=0, has_side_effects=True, vmem_limit_bytes=62 * 1024 * 1024
        ),
        name="routed_ffn",
    )(
        live_rows, tokens, norm_gain.reshape(1, D), router.T, expert_ids, w_gate, w_up, w_down
    )


def solution(mesh):
    return jax.shard_map(
        local,
        mesh=mesh,
        in_specs=(
            P(("groups", "expert"), None),
            P(),
            P(),
            P(None, "expert"),
            P(None, "expert"),
            P("expert", None),
            P(("groups", "expert"), None),
            P(("groups", "expert")),
        ),
        out_specs=P(("groups", "expert"), None),
        check_vma=False,
    )
```

```python
import functools

import jax
import jax.numpy as jnp
from jax import lax
from jax.experimental import pallas as pl
from jax.experimental.pallas import tpu as pltpu
from jax.sharding import PartitionSpec as P

EPS = 1e-05
LANES = 128
GATHER_CHUNKS = 3
REDUCE_CHUNKS = 4
ROW_BLOCK = 128
CORES = 2


def _mod(a, n):
    return lax.rem(a + n, n)


def kernel(
    E, Q, B, D, H,
    live_ref, tok_hbm, gain_hbm, router_hbm, ids_hbm, wg_hbm, wu_hbm, wd_hbm,
    out_ref,
    tok_ref, gain_ref, router_ref, ids_ref, G, wg, wu, wd, acc_g, acc_u, hid, part, core_in, chip_sum, quad_in, plane, plane_in,
    load_sem, az_send, az_recv, aq_send, aq_recv, ac_send, ac_recv,
    rc_send, rc_recv, rq_send, rq_recv, rz_send, rz_recv,
):
    me = lax.axis_index("expert")
    members = Q * CORES
    e = me // members
    m = lax.rem(me, members)
    q = m // CORES
    c = lax.rem(m, CORES)
    rows = CORES * Q * E * B
    half = Q * E * B
    quad = E * B

    def dev(e_, q_, c_):
        return {"expert": (e_ * Q + q_) * CORES + c_}

    def slot(e_, q_, c_):
        return (c_ * Q + q_) * E + e_

    def remote(src, dst, ssem, rsem, device):
        return pltpu.make_async_remote_copy(
            src_ref=src, dst_ref=dst, send_sem=ssem, recv_sem=rsem,
            device_id=device, device_id_type=pl.DeviceIdType.MESH,
        )

    def wait_bytes(ref, sem):
        pltpu.make_async_copy(ref, ref, sem).wait()

    barrier = pltpu.get_barrier_semaphore()
    others_e = [_mod(e + d, E) for d in range(1, E)]
    others_q = [_mod(q + d, Q) for d in range(1, Q)]
    for e2 in others_e:
        pl.semaphore_signal(barrier, inc=1, device_id=dev(e2, q, c), device_id_type=pl.DeviceIdType.MESH)
    for q2 in others_q:
        pl.semaphore_signal(barrier, inc=1, device_id=dev(e, q2, c), device_id_type=pl.DeviceIdType.MESH)
    pl.semaphore_signal(barrier, inc=1, device_id=dev(e, q, 1 - c), device_id_type=pl.DeviceIdType.MESH)

    tok_load = pltpu.make_async_copy(tok_hbm, tok_ref, load_sem.at[0])
    wg_load = pltpu.make_async_copy(wg_hbm, wg, load_sem.at[1])
    wu_load = pltpu.make_async_copy(wu_hbm, wu, load_sem.at[2])
    wd_load = pltpu.make_async_copy(wd_hbm, wd, load_sem.at[3])
    gain_load = pltpu.make_async_copy(gain_hbm, gain_ref, load_sem.at[4])
    router_load = pltpu.make_async_copy(router_hbm, router_ref, load_sem.at[5])
    ids_load = pltpu.make_async_copy(ids_hbm, ids_ref, load_sem.at[6])
    for load in (tok_load, gain_load, router_load, ids_load, wg_load, wu_load, wd_load):
        load.start()
    tok_load.wait()
    gain_load.wait()

    tok = tok_ref[...].astype(jnp.float32)
    scale = lax.rsqrt(jnp.sum(tok * tok, axis=-1, keepdims=True) * (1.0 / D) + EPS)
    normed = (tok * scale * gain_ref[...]).astype(jnp.bfloat16)
    mine = slot(e, q, c)
    G[mine, :, :D] = normed

    pl.semaphore_wait(barrier, (E - 1) + (Q - 1) + 1)

    step = D // GATHER_CHUNKS
    spans = [
        pl.ds(j * step, step + (LANES if j == GATHER_CHUNKS - 1 else 0))
        for j in range(GATHER_CHUNKS)
    ]

    def send_experts(j):
        for d in range(1, E):
            view = G.at[mine, :, spans[j]]
            remote(view, view, az_send, az_recv.at[j, d - 1], dev(others_e[d - 1], q, c)).start()
        for dq in range(1, Q):
            view = G.at[mine, :, spans[j]]
            remote(view, view, aq_send, aq_recv.at[j, dq - 1], dev(e, others_q[dq - 1], c)).start()

    for j in range(GATHER_CHUNKS - 1):
        send_experts(j)

    normed_f = normed.astype(jnp.float32)
    router_load.wait()
    ids_load.wait()
    router = router_ref[...].astype(jnp.float32)
    ids = ids_ref[...]
    diagonal = lax.broadcasted_iota(jnp.int32, (B, B), 0) == lax.broadcasted_iota(jnp.int32, (B, B), 1)
    first_id = jnp.sum(jnp.where(diagonal, ids[0:1, :], 0), axis=-1, keepdims=True)
    second_id = jnp.sum(jnp.where(diagonal, ids[1:2, :], 0), axis=-1, keepdims=True)
    first = jnp.zeros((B, 1), jnp.float32)
    second = jnp.zeros((B, 1), jnp.float32)
    for k in range(E):
        logit = jnp.sum(normed_f * router[k : k + 1, :], axis=-1, keepdims=True)
        first = jnp.where(first_id == k, logit, first)
        second = jnp.where(second_id == k, logit, second)
    row_at = lax.broadcasted_iota(jnp.int32, (B, 1), 0)
    alive = jnp.where(row_at < live_ref[0], 1.0, 0.0).astype(jnp.float32)
    gate0 = alive * jax.nn.sigmoid(first - second)
    gate1 = alive * jax.nn.sigmoid(second - first)
    lane = lax.broadcasted_iota(jnp.int32, (B, LANES), 1)
    low_lane = lane - E
    weight = jnp.where(first_id == lane, gate0, 0.0) + jnp.where(second_id == lane, gate1, 0.0)
    again = jnp.where(first_id == low_lane, gate0, 0.0) + jnp.where(second_id == low_lane, gate1, 0.0)
    low = again - again.astype(jnp.bfloat16).astype(jnp.float32)
    G[mine, :, pl.ds(D, LANES)] = (weight + low).astype(jnp.bfloat16)
    send_experts(GATHER_CHUNKS - 1)

    def gather_a(j):
        for d in range(1, E):
            s = slot(_mod(e - d, E), q, c)
            view = G.at[s, :, spans[j]]
            remote(view, view, az_send, az_recv.at[j, d - 1], dev(e, q, c)).wait_recv()
            for dq in range(1, Q):
                remote(view, view, aq_send, aq_recv.at[j, dq - 1], dev(e, others_q[dq - 1], c)).start()
        view = G.at[pl.ds(slot(0, q, c), E), :, spans[j]]
        remote(view, view, ac_send, ac_recv.at[j, 0], dev(e, q, 1 - c)).start()

    def gather_b(j):
        for dq in range(1, Q):
            view = G.at[pl.ds(slot(0, _mod(q - dq, Q), c), E), :, spans[j]]
            wait_bytes(view, aq_recv.at[j, dq - 1])
            remote(view, view, ac_send, ac_recv.at[j, dq], dev(e, q, 1 - c)).start()

    blocks = max(1, rows // ROW_BLOCK)
    block = rows // blocks

    def over_rows(body):
        if blocks == 1:
            body(0)
        else:
            lax.fori_loop(0, blocks, lambda i, _: (body(i), 0)[1], 0)

    def lhs(i, at, width):
        view = G[pl.ds(i * (block // B), block // B), :, pl.ds(at, width)]
        return view.astype(jnp.float32).reshape(block, width)

    def gather_c(j):
        for dq in range(Q):
            view = G.at[pl.ds(slot(0, _mod(q - dq, Q), 1 - c), E), :, spans[j]]
            wait_bytes(view, ac_recv.at[j, dq])
        if j == 0:
            wg_load.wait()
            wu_load.wait()

        def body(i):
            at = pl.ds(i * block, block)
            x = lhs(i, j * step, step).astype(jnp.bfloat16)
            g = jnp.dot(x, wg[pl.ds(j * step, step), :], preferred_element_type=jnp.float32)
            u = jnp.dot(x, wu[pl.ds(j * step, step), :], preferred_element_type=jnp.float32)
            if j:
                g = g + acc_g[at, :]
                u = u + acc_u[at, :]
            if j < GATHER_CHUNKS - 1:
                acc_g[at, :] = g
                acc_u[at, :] = u
            else:
                coded = lhs(i, D, LANES)
                lanes = lax.broadcasted_iota(jnp.int32, coded.shape, 1)
                keep = (lanes == e) | (lanes == e + E)
                w = jnp.sum(jnp.where(keep, coded, 0.0), axis=-1, keepdims=True)
                hid[at, :] = (g / (1.0 + jnp.exp(-g)) * u * w).astype(jnp.bfloat16)

        over_rows(body)

    for t in range(GATHER_CHUNKS + 2):
        if t < GATHER_CHUNKS:
            gather_a(t)
        if 0 <= t - 1 < GATHER_CHUNKS:
            gather_b(t - 1)
        if 0 <= t - 2 < GATHER_CHUNKS:
            gather_c(t - 2)

    wd_load.wait()
    width = D // REDUCE_CHUNKS

    def at_rows(start, size):
        return pl.ds(pl.multiple_of(start, 16), size)

    def reduce_a(j):
        cols = pl.ds(j * width, width)

        def body(i):
            at = pl.ds(i * block, block)
            part[at, cols] = jnp.dot(
                hid[at, :], wd[:, cols], preferred_element_type=jnp.float32
            ).astype(jnp.bfloat16)

        over_rows(body)
        remote(
            part.at[at_rows((1 - c) * half, half), cols], core_in.at[:, cols],
            rc_send, rc_recv.at[j], dev(e, q, 1 - c),
        ).start()

    def reduce_b(j):
        cols = pl.ds(j * width, width)
        wait_bytes(core_in.at[:, cols], rc_recv.at[j])
        for d in list(range(1, Q)) + [0]:
            q2 = _mod(q + d, Q)
            at = at_rows(q2 * quad, quad)
            own = part[at_rows(c * half + q2 * quad, quad), cols].astype(jnp.float32)
            chip_sum[at, cols] = (own + core_in[at, cols].astype(jnp.float32)).astype(jnp.bfloat16)
            if d:
                remote(
                    chip_sum.at[at, cols], quad_in.at[d - 1, :, cols],
                    rq_send, rq_recv.at[j, d - 1], dev(e, q2, c),
                ).start()

    def reduce_c(j):
        cols = pl.ds(j * width, width)
        total = chip_sum[at_rows(q * quad, quad), cols].astype(jnp.float32)
        for d in range(1, Q):
            wait_bytes(quad_in.at[d - 1, :, cols], rq_recv.at[j, d - 1])
            total = total + quad_in[d - 1, :, cols].astype(jnp.float32)
        plane[:, :, cols] = total.reshape(E, B, width).astype(jnp.bfloat16)
        for d in range(1, E):
            remote(
                plane.at[others_e[d - 1], :, cols], plane_in.at[d - 1, :, cols],
                rz_send, rz_recv.at[j, d - 1], dev(others_e[d - 1], q, c),
            ).start()

    def reduce_d(j):
        cols = pl.ds(j * width, width)
        total = tok_ref[:, cols].astype(jnp.float32) + plane[e, :, cols].astype(jnp.float32)
        for d in range(1, E):
            wait_bytes(plane_in.at[d - 1, :, cols], rz_recv.at[j, d - 1])
            total = total + plane_in[d - 1, :, cols].astype(jnp.float32)
        out_ref[:, cols] = total.astype(jnp.bfloat16)

    for t in range(REDUCE_CHUNKS + 1):
        if t < REDUCE_CHUNKS:
            reduce_a(t)
        if t:
            reduce_b(t - 1)
    for stage in (reduce_c, reduce_d):
        for t in range(REDUCE_CHUNKS):
            stage(t)

    wait_bytes(G.at[pl.ds(0, E - 1)], az_send)
    if Q > 1:
        wait_bytes(G.at[pl.ds(0, (Q - 1) * E)], aq_send)
    wait_bytes(G.at[pl.ds(0, Q * E)], ac_send)
    wait_bytes(core_in, rc_send)
    if Q > 1:
        wait_bytes(quad_in, rq_send)
    wait_bytes(plane_in, rz_send)


def local(tokens, norm_gain, router, w_gate, w_up, w_down, expert_ids, live_rows):
    devices = lax.axis_size("expert")
    B, D = tokens.shape
    E = router.shape[1]
    H = w_gate.shape[1]
    Q = devices // E // CORES
    rows = devices * B
    bf = jnp.bfloat16
    vmem = pl.BlockSpec(memory_space=pltpu.VMEM)
    anyspace = pl.BlockSpec(memory_space=pl.ANY)
    dma = pltpu.SemaphoreType.DMA
    return pl.pallas_call(
        functools.partial(kernel, E, Q, B, D, H),
        out_shape=jax.ShapeDtypeStruct((B, D), bf),
        in_specs=[
            pl.BlockSpec(memory_space=pltpu.SMEM),
            anyspace, anyspace, anyspace, anyspace, anyspace, anyspace, anyspace,
        ],
        out_specs=vmem,
        scratch_shapes=[
            pltpu.VMEM((B, D), bf),
            pltpu.VMEM((1, D), jnp.float32),
            pltpu.VMEM((E, D), bf),
            pltpu.VMEM((2, B), jnp.int32),
            pltpu.VMEM((devices, B, D + LANES), bf),
            pltpu.VMEM((D, H), bf),
            pltpu.VMEM((D, H), bf),
            pltpu.VMEM((H, D), bf),
            pltpu.VMEM((rows, H), jnp.float32),
            pltpu.VMEM((rows, H), jnp.float32),
            pltpu.VMEM((rows, H), bf),
            pltpu.VMEM((rows, D), bf),
            pltpu.VMEM((Q * E * B, D), bf),
            pltpu.VMEM((Q * E * B, D), bf),
            pltpu.VMEM((max(Q - 1, 1), E * B, D), bf),
            pltpu.VMEM((E, B, D), bf),
            pltpu.VMEM((E - 1, B, D), bf),
            dma((7,)),
            dma, dma((GATHER_CHUNKS, E - 1)),
            dma, dma((GATHER_CHUNKS, max(Q - 1, 1))),
            dma, dma((GATHER_CHUNKS, Q)),
            dma, dma((REDUCE_CHUNKS,)),
            dma, dma((REDUCE_CHUNKS, max(Q - 1, 1))),
            dma, dma((REDUCE_CHUNKS, E - 1)),
        ],
        compiler_params=pltpu.CompilerParams(
            collective_id=0, has_side_effects=True, vmem_limit_bytes=62 * 1024 * 1024
        ),
        name="routed_ffn",
    )(
        live_rows, tokens, norm_gain.reshape(1, D), router.T, expert_ids.T, w_gate, w_up, w_down
    )


def solution(mesh):
    return jax.shard_map(
        local,
        mesh=mesh,
        in_specs=(
            P(("groups", "expert"), None),
            P(),
            P(),
            P(None, "expert"),
            P(None, "expert"),
            P("expert", None),
            P(("groups", "expert"), None),
            P(("groups", "expert")),
        ),
        out_specs=P(("groups", "expert"), None),
        check_vma=False,
    )
```

```python
import functools

import jax
import jax.numpy as jnp
from jax import lax
from jax.experimental import pallas as pl
from jax.experimental.pallas import tpu as pltpu
from jax.sharding import PartitionSpec as P

EPS = 1e-05
LANES = 128
GATHER_CHUNKS = 3
REDUCE_CHUNKS = 6
ROW_BLOCK = 128
CORES = 2


def _mod(a, n):
    return lax.rem(a + n, n)


def kernel(
    E, Q, B, D, H,
    live_ref, tok_hbm, gain_hbm, router_hbm, ids_hbm, wg_hbm, wu_hbm, wd_hbm,
    out_ref,
    tok_ref, gain_ref, router_ref, ids_ref, G, wg, wu, wd, acc_g, acc_u, hid, part, core_in, chip_sum, quad_in, plane, plane_in,
    load_sem, az_send, az_recv, aq_send, aq_recv, ac_send, ac_recv,
    rc_send, rc_recv, rq_send, rq_recv, rz_send, rz_recv,
):
    me = lax.axis_index("expert")
    members = Q * CORES
    e = me // members
    m = lax.rem(me, members)
    q = m // CORES
    c = lax.rem(m, CORES)
    rows = CORES * Q * E * B
    half = Q * E * B
    quad = E * B

    def dev(e_, q_, c_):
        return {"expert": (e_ * Q + q_) * CORES + c_}

    def slot(e_, q_, c_):
        return (c_ * Q + q_) * E + e_

    def remote(src, dst, ssem, rsem, device):
        return pltpu.make_async_remote_copy(
            src_ref=src, dst_ref=dst, send_sem=ssem, recv_sem=rsem,
            device_id=device, device_id_type=pl.DeviceIdType.MESH,
        )

    def wait_bytes(ref, sem):
        pltpu.make_async_copy(ref, ref, sem).wait()

    barrier = pltpu.get_barrier_semaphore()
    others_e = [_mod(e + d, E) for d in range(1, E)]
    others_q = [_mod(q + d, Q) for d in range(1, Q)]
    for e2 in others_e:
        pl.semaphore_signal(barrier, inc=1, device_id=dev(e2, q, c), device_id_type=pl.DeviceIdType.MESH)
    for q2 in others_q:
        pl.semaphore_signal(barrier, inc=1, device_id=dev(e, q2, c), device_id_type=pl.DeviceIdType.MESH)
    pl.semaphore_signal(barrier, inc=1, device_id=dev(e, q, 1 - c), device_id_type=pl.DeviceIdType.MESH)

    tok_load = pltpu.make_async_copy(tok_hbm, tok_ref, load_sem.at[0])
    wg_load = pltpu.make_async_copy(wg_hbm, wg, load_sem.at[1])
    wu_load = pltpu.make_async_copy(wu_hbm, wu, load_sem.at[2])
    wd_load = pltpu.make_async_copy(wd_hbm, wd, load_sem.at[3])
    gain_load = pltpu.make_async_copy(gain_hbm, gain_ref, load_sem.at[4])
    router_load = pltpu.make_async_copy(router_hbm, router_ref, load_sem.at[5])
    ids_load = pltpu.make_async_copy(ids_hbm, ids_ref, load_sem.at[6])
    for load in (tok_load, gain_load, router_load, ids_load, wg_load, wu_load, wd_load):
        load.start()
    tok_load.wait()
    gain_load.wait()

    tok = tok_ref[...].astype(jnp.float32)
    scale = lax.rsqrt(jnp.sum(tok * tok, axis=-1, keepdims=True) * (1.0 / D) + EPS)
    normed = (tok * scale * gain_ref[...]).astype(jnp.bfloat16)
    mine = slot(e, q, c)
    G[mine, :, :D] = normed


    step = D // GATHER_CHUNKS
    spans = [
        pl.ds(j * step, step + (LANES if j == GATHER_CHUNKS - 1 else 0))
        for j in range(GATHER_CHUNKS)
    ]

    def send_experts(j):
        for d in range(1, E):
            view = G.at[mine, :, spans[j]]
            remote(view, view, az_send, az_recv.at[j, d - 1], dev(others_e[d - 1], q, c)).start()
        for dq in range(1, Q):
            view = G.at[mine, :, spans[j]]
            remote(view, view, aq_send, aq_recv.at[j, dq - 1], dev(e, others_q[dq - 1], c)).start()


    normed_f = normed.astype(jnp.float32)
    router_load.wait()
    ids_load.wait()
    router = router_ref[...].astype(jnp.float32)
    ids = ids_ref[...]
    diagonal = lax.broadcasted_iota(jnp.int32, (B, B), 0) == lax.broadcasted_iota(jnp.int32, (B, B), 1)
    first_id = jnp.sum(jnp.where(diagonal, ids[0:1, :], 0), axis=-1, keepdims=True)
    second_id = jnp.sum(jnp.where(diagonal, ids[1:2, :], 0), axis=-1, keepdims=True)
    first = jnp.zeros((B, 1), jnp.float32)
    second = jnp.zeros((B, 1), jnp.float32)
    for k in range(E):
        logit = jnp.sum(normed_f * router[k : k + 1, :], axis=-1, keepdims=True)
        first = jnp.where(first_id == k, logit, first)
        second = jnp.where(second_id == k, logit, second)
    row_at = lax.broadcasted_iota(jnp.int32, (B, 1), 0)
    alive = jnp.where(row_at < live_ref[0], 1.0, 0.0).astype(jnp.float32)
    gate0 = alive * jax.nn.sigmoid(first - second)
    gate1 = alive * jax.nn.sigmoid(second - first)
    lane = lax.broadcasted_iota(jnp.int32, (B, LANES), 1)
    low_lane = lane - E
    weight = jnp.where(first_id == lane, gate0, 0.0) + jnp.where(second_id == lane, gate1, 0.0)
    again = jnp.where(first_id == low_lane, gate0, 0.0) + jnp.where(second_id == low_lane, gate1, 0.0)
    low = again - again.astype(jnp.bfloat16).astype(jnp.float32)
    G[mine, :, pl.ds(D, LANES)] = (weight + low).astype(jnp.bfloat16)
    pl.semaphore_wait(barrier, (E - 1) + (Q - 1) + 1)
    for j in range(GATHER_CHUNKS):
        send_experts(j)

    def gather_a(j):
        for d in range(1, E):
            s = slot(_mod(e - d, E), q, c)
            view = G.at[s, :, spans[j]]
            remote(view, view, az_send, az_recv.at[j, d - 1], dev(e, q, c)).wait_recv()
            for dq in range(1, Q):
                remote(view, view, aq_send, aq_recv.at[j, dq - 1], dev(e, others_q[dq - 1], c)).start()
        view = G.at[pl.ds(slot(0, q, c), E), :, spans[j]]
        remote(view, view, ac_send, ac_recv.at[j, 0], dev(e, q, 1 - c)).start()

    def gather_b(j):
        for dq in range(1, Q):
            view = G.at[pl.ds(slot(0, _mod(q - dq, Q), c), E), :, spans[j]]
            wait_bytes(view, aq_recv.at[j, dq - 1])
            remote(view, view, ac_send, ac_recv.at[j, dq], dev(e, q, 1 - c)).start()

    blocks = max(1, rows // ROW_BLOCK)
    block = rows // blocks

    def over_rows(body):
        if blocks == 1:
            body(0)
        else:
            lax.fori_loop(0, blocks, lambda i, _: (body(i), 0)[1], 0)

    def lhs(i, at, width):
        view = G[pl.ds(i * (block // B), block // B), :, pl.ds(at, width)]
        return view.astype(jnp.float32).reshape(block, width)

    def gather_c(j):
        for dq in range(Q):
            view = G.at[pl.ds(slot(0, _mod(q - dq, Q), 1 - c), E), :, spans[j]]
            wait_bytes(view, ac_recv.at[j, dq])
        if j == 0:
            wg_load.wait()
            wu_load.wait()

        def body(i):
            at = pl.ds(i * block, block)
            x = lhs(i, j * step, step).astype(jnp.bfloat16)
            g = jnp.dot(x, wg[pl.ds(j * step, step), :], preferred_element_type=jnp.float32)
            u = jnp.dot(x, wu[pl.ds(j * step, step), :], preferred_element_type=jnp.float32)
            if j:
                g = g + acc_g[at, :]
                u = u + acc_u[at, :]
            if j < GATHER_CHUNKS - 1:
                acc_g[at, :] = g
                acc_u[at, :] = u
            else:
                coded = lhs(i, D, LANES)
                lanes = lax.broadcasted_iota(jnp.int32, coded.shape, 1)
                keep = (lanes == e) | (lanes == e + E)
                w = jnp.sum(jnp.where(keep, coded, 0.0), axis=-1, keepdims=True)
                hid[at, :] = (g / (1.0 + jnp.exp(-g)) * u * w).astype(jnp.bfloat16)

        over_rows(body)

    for t in range(GATHER_CHUNKS + 2):
        if t < GATHER_CHUNKS:
            gather_a(t)
        if 0 <= t - 1 < GATHER_CHUNKS:
            gather_b(t - 1)
        if 0 <= t - 2 < GATHER_CHUNKS:
            gather_c(t - 2)

    wd_load.wait()
    width = D // REDUCE_CHUNKS

    def at_rows(start, size):
        return pl.ds(pl.multiple_of(start, 16), size)

    def reduce_a(j):
        cols = pl.ds(j * width, width)

        def body(i):
            at = pl.ds(i * block, block)
            part[at, cols] = jnp.dot(
                hid[at, :], wd[:, cols], preferred_element_type=jnp.float32
            ).astype(jnp.bfloat16)

        over_rows(body)
        remote(
            part.at[at_rows((1 - c) * half, half), cols], core_in.at[:, cols],
            rc_send, rc_recv.at[j], dev(e, q, 1 - c),
        ).start()

    def reduce_b(j):
        cols = pl.ds(j * width, width)
        wait_bytes(core_in.at[:, cols], rc_recv.at[j])
        for d in list(range(1, Q)) + [0]:
            q2 = _mod(q + d, Q)
            at = at_rows(q2 * quad, quad)
            own = part[at_rows(c * half + q2 * quad, quad), cols].astype(jnp.float32)
            chip_sum[at, cols] = (own + core_in[at, cols].astype(jnp.float32)).astype(jnp.bfloat16)
            if d:
                remote(
                    chip_sum.at[at, cols], quad_in.at[d - 1, :, cols],
                    rq_send, rq_recv.at[j, d - 1], dev(e, q2, c),
                ).start()

    def reduce_c(j):
        cols = pl.ds(j * width, width)
        total = chip_sum[at_rows(q * quad, quad), cols].astype(jnp.float32)
        for d in range(1, Q):
            wait_bytes(quad_in.at[d - 1, :, cols], rq_recv.at[j, d - 1])
            total = total + quad_in[d - 1, :, cols].astype(jnp.float32)
        plane[:, :, cols] = total.reshape(E, B, width).astype(jnp.bfloat16)
        for d in range(1, E):
            remote(
                plane.at[others_e[d - 1], :, cols], plane_in.at[d - 1, :, cols],
                rz_send, rz_recv.at[j, d - 1], dev(others_e[d - 1], q, c),
            ).start()

    def reduce_d(j):
        cols = pl.ds(j * width, width)
        total = tok_ref[:, cols].astype(jnp.float32) + plane[e, :, cols].astype(jnp.float32)
        for d in range(1, E):
            wait_bytes(plane_in.at[d - 1, :, cols], rz_recv.at[j, d - 1])
            total = total + plane_in[d - 1, :, cols].astype(jnp.float32)
        out_ref[:, cols] = total.astype(jnp.bfloat16)

    for t in range(REDUCE_CHUNKS + 1):
        if t < REDUCE_CHUNKS:
            reduce_a(t)
        if t:
            reduce_b(t - 1)
    for stage in (reduce_c, reduce_d):
        for t in range(REDUCE_CHUNKS):
            stage(t)

    wait_bytes(G.at[pl.ds(0, E - 1)], az_send)
    if Q > 1:
        wait_bytes(G.at[pl.ds(0, (Q - 1) * E)], aq_send)
    wait_bytes(G.at[pl.ds(0, Q * E)], ac_send)
    wait_bytes(core_in, rc_send)
    if Q > 1:
        wait_bytes(quad_in, rq_send)
    wait_bytes(plane_in, rz_send)


def local(tokens, norm_gain, router, w_gate, w_up, w_down, expert_ids, live_rows):
    devices = lax.axis_size("expert")
    B, D = tokens.shape
    E = router.shape[1]
    H = w_gate.shape[1]
    Q = devices // E // CORES
    rows = devices * B
    bf = jnp.bfloat16
    vmem = pl.BlockSpec(memory_space=pltpu.VMEM)
    anyspace = pl.BlockSpec(memory_space=pl.ANY)
    dma = pltpu.SemaphoreType.DMA
    return pl.pallas_call(
        functools.partial(kernel, E, Q, B, D, H),
        out_shape=jax.ShapeDtypeStruct((B, D), bf),
        in_specs=[
            pl.BlockSpec(memory_space=pltpu.SMEM),
            anyspace, anyspace, anyspace, anyspace, anyspace, anyspace, anyspace,
        ],
        out_specs=vmem,
        scratch_shapes=[
            pltpu.VMEM((B, D), bf),
            pltpu.VMEM((1, D), jnp.float32),
            pltpu.VMEM((E, D), bf),
            pltpu.VMEM((2, B), jnp.int32),
            pltpu.VMEM((devices, B, D + LANES), bf),
            pltpu.VMEM((D, H), bf),
            pltpu.VMEM((D, H), bf),
            pltpu.VMEM((H, D), bf),
            pltpu.VMEM((rows, H), jnp.float32),
            pltpu.VMEM((rows, H), jnp.float32),
            pltpu.VMEM((rows, H), bf),
            pltpu.VMEM((rows, D), bf),
            pltpu.VMEM((Q * E * B, D), bf),
            pltpu.VMEM((Q * E * B, D), bf),
            pltpu.VMEM((max(Q - 1, 1), E * B, D), bf),
            pltpu.VMEM((E, B, D), bf),
            pltpu.VMEM((E - 1, B, D), bf),
            dma((7,)),
            dma, dma((GATHER_CHUNKS, E - 1)),
            dma, dma((GATHER_CHUNKS, max(Q - 1, 1))),
            dma, dma((GATHER_CHUNKS, Q)),
            dma, dma((REDUCE_CHUNKS,)),
            dma, dma((REDUCE_CHUNKS, max(Q - 1, 1))),
            dma, dma((REDUCE_CHUNKS, E - 1)),
        ],
        compiler_params=pltpu.CompilerParams(
            collective_id=0, has_side_effects=True, vmem_limit_bytes=62 * 1024 * 1024
        ),
        name="routed_ffn",
    )(
        live_rows, tokens, norm_gain.reshape(1, D), router.T, expert_ids.T, w_gate, w_up, w_down
    )


def solution(mesh):
    return jax.shard_map(
        local,
        mesh=mesh,
        in_specs=(
            P(("groups", "expert"), None),
            P(),
            P(),
            P(None, "expert"),
            P(None, "expert"),
            P("expert", None),
            P(("groups", "expert"), None),
            P(("groups", "expert")),
        ),
        out_specs=P(("groups", "expert"), None),
        check_vma=False,
    )
```
